32 devices in a mesh: row: 4 (over z), col: 8 (over y, x, core).
Axes of the slice: x: 2, y: 2, z: 4, core: 2. Of those that a mesh axis runs over, the one named last changes fastest.
Arguments:
- child_inverse: bfloat16 [28672, 14336], P('row', 'col'), as said below
- root_upper: bfloat16 [20480, 20480], P('row', 'col'), as said below
- coupling: bfloat16 [4096, 28672], P('col', 'row'), may hold values from -0.046875 to 0.046875
- child_rhs: float32 [14336, 2, 128], P('col'), may hold values from -6 to 6
- root_rhs: float32 [20480, 128], P(('row', 'col')), may hold values from -6 to 6
- child_map: int32 [2, 32], replicated, may hold values from 0 to 159, as said below
Outputs:
- root_solution: float32 [20480, 128], P(('row', 'col'))
- child_solution: float32 [14336, 2, 128], P('col')
The draws below stay inside these ranges and needn't reach their ends.
Inputs may be any that keep to these rules, and one draw needn't show every extreme that they name: `child_inverse`: for each child k, rows k * 14336 to (k + 1) * 14336 - 1 hold a lower triangular matrix: zero above the diagonal, diagonal entries between 0.5 and 1.5. `root_upper`: an upper triangular matrix: zero below the diagonal, diagonal entries between 0.5 and 1.5. `child_map`: each row lists 4096 / 128 distinct root blocks in increasing order, beginning with block 0 and ending with block 159.
All inputs are finite; a program needn't handle non-finite values.
Results may differ from the reference program's by a relative error of at most 0.018.
Values may be sent and summed in bfloat16 or wider, within the bound.
A program may use at most 192 MiB of HBM per device.

```python
import math
import jax
import jax.numpy as jnp
from jax import lax

S0 = 20480
S1 = 14336
U = 4096
NRHS = 128
BLK = 128


def triangle_draw(key, shape, order, lower):
    noise_key = jax.random.fold_in(key, 11)
    diag_key = jax.random.fold_in(key, 12)
    row_ids = lax.broadcasted_iota(jnp.int32, shape, 0) % order
    col_ids = lax.broadcasted_iota(jnp.int32, shape, 1)
    noise = jax.random.normal(noise_key, shape, jnp.float32)
    noise = noise * (1.0 / math.sqrt(order))
    diagonal = jax.random.uniform(diag_key, (shape[0], 1), jnp.float32, 0.5, 1.5)
    if lower:
        inside = row_ids > col_ids
    else:
        inside = row_ids < col_ids
    return jnp.where(inside, noise, jnp.where(row_ids == col_ids, diagonal, 0.0))


def draw_child_inverse(key, part):
    return triangle_draw(key, (2 * S1, S1), S1, True).astype(jnp.bfloat16)


def draw_root_upper(key, part):
    return triangle_draw(key, (S0, S0), S0, False).astype(jnp.bfloat16)


def draw_child_map(key, part):
    map_rows = []
    for member in range(2):
        middle = jax.random.permutation(jax.random.fold_in(key, 21 + member), S0 // BLK - 2)[:U // BLK - 2] + 1
        ordered = jnp.sort(middle.astype(jnp.int32))
        first_block = jnp.zeros((1,), jnp.int32)
        last_block = jnp.full((1,), S0 // BLK - 1, jnp.int32)
        map_rows.append(jnp.concatenate([first_block, ordered, last_block]))
    return jnp.stack(map_rows)


def block_levels(stream_key, dims, split, smallest, top_value):
    gain = 1.0
    for dim, parts in split:
        steps = jax.random.uniform(jax.random.fold_in(jax.random.fold_in(stream_key, 6), dim), (parts,), jnp.float32, smallest / len(split), top_value / len(split))
        gain = gain * jnp.repeat(jnp.exp(steps), dims[dim] // parts).reshape((-1,) + (1,) * (len(dims) - 1 - dim))
    return gain


def scatter_about(key, shape, spread, most, pieces=(), dtype=jnp.bfloat16):
    drawn = jax.random.normal(key, shape, jnp.float32) * spread
    if len(pieces) > 0:
        drawn = block_levels(key, shape, pieces, -0.22, 0.18) * drawn
    return jnp.clip(drawn, min=-most, max=most).astype(dtype)


def setup_inputs(seed: int = 0) -> dict:
    key_of = jax.random.split(jax.random.key(seed), 7)
    child_inverse = draw_child_inverse(jax.random.fold_in(key_of[6], 71), 0)
    root_upper = draw_root_upper(jax.random.fold_in(key_of[6], 71), 0)
    coupling = scatter_about(key_of[2], (U, 2 * S1), S1 ** -0.5, 0.046875, ((0, 8), (1, 4)))
    child_rhs = scatter_about(key_of[3], (S1, 2, NRHS), 1.0, 6.0, ((0, 8),), jnp.float32)
    root_rhs = scatter_about(key_of[4], (S0, NRHS), 1.0, 6.0, ((0, 32),), jnp.float32)
    child_map = draw_child_map(jax.random.fold_in(key_of[6], 71), 0)
    return dict(child_inverse=child_inverse, root_upper=root_upper, coupling=coupling, child_rhs=child_rhs, root_rhs=root_rhs, child_map=child_map)


def reference(child_inverse, root_upper, coupling, child_rhs, root_rhs, child_map):
    rhs_low = child_rhs.astype(jnp.bfloat16)
    root_blocks = S0 // BLK
    update_sum = jnp.zeros((root_blocks, BLK, NRHS), jnp.float32)
    solved_list = []
    for member in range(2):
        inverse = child_inverse[member * S1:(member + 1) * S1]
        part_coupling = coupling[:, member * S1:(member + 1) * S1]
        child_solved = jnp.dot(inverse, rhs_low[:, member, :], preferred_element_type=jnp.float32)
        update = jnp.dot(part_coupling, child_solved.astype(jnp.bfloat16), preferred_element_type=jnp.float32)
        update_sum = update_sum.at[child_map[member]].add(update.reshape(U // BLK, BLK, NRHS))
        solved_list.append(child_solved)
    root_changed = root_rhs - update_sum.reshape(S0, NRHS)
    root_low = root_changed.astype(jnp.bfloat16)
    root_solved = jnp.dot(root_upper.T, root_low, preferred_element_type=jnp.float32)
    solved_low = root_solved.astype(jnp.bfloat16)
    root_solution = jnp.dot(root_upper, solved_low, preferred_element_type=jnp.float32)
    rows_low = root_solution.astype(jnp.bfloat16).reshape(root_blocks, BLK, NRHS)
    final_list = []
    for member in range(2):
        inverse = child_inverse[member * S1:(member + 1) * S1]
        part_coupling = coupling[:, member * S1:(member + 1) * S1]
        picked = rows_low[child_map[member]].reshape(U, NRHS)
        back_term = jnp.dot(part_coupling.T, picked, preferred_element_type=jnp.float32)
        adjusted = (solved_list[member] - back_term).astype(jnp.bfloat16)
        final_list.append(jnp.dot(inverse.T, adjusted, preferred_element_type=jnp.float32))
    return root_solution, jnp.stack(final_list, axis=1)
```

```python
import functools

import jax
import jax.numpy as jnp
from jax import lax
from jax.experimental import pallas as pl
from jax.experimental.pallas import tpu as pltpu
from jax.sharding import PartitionSpec as P

BLK = 128
MESH = pl.DeviceIdType.MESH


def bits_of(n):
    m = n.bit_length() - 1
    assert 1 << m == n
    return m


def greet(axis, me, bits):
    barrier = pltpu.get_barrier_semaphore()
    for b in bits:
        pl.semaphore_signal(
            barrier, inc=1, device_id={axis: me ^ (1 << b)}, device_id_type=MESH
        )
    pl.semaphore_wait(barrier, len(bits))


def remote(axis, me, bit, src, dst, send, recv):
    copy = pltpu.make_async_remote_copy(
        src_ref=src,
        dst_ref=dst,
        send_sem=send,
        recv_sem=recv,
        device_id={axis: me ^ (1 << bit)},
        device_id_type=MESH,
    )
    copy.start()
    return copy


def scatter_steps(axis, me, orders, n, x_ref, w_ref, r_ref, put, send, recv):
    streams = len(orders)
    steps = len(orders[0])
    low = [jnp.int32(0)] * streams
    size = n
    offset = 0
    copies = []
    for t in range(steps):
        half = size // 2
        src = x_ref if t == 0 else w_ref
        now = []
        for s in range(streams):
            mine = (me >> orders[s][t]) & 1
            keep = low[s] + mine * half
            away = low[s] + (1 - mine) * half
            copy = remote(
                axis,
                me,
                orders[s][t],
                src.at[s, pl.ds(away, half)],
                r_ref.at[s, pl.ds(offset, half)],
                send.at[s, t],
                recv.at[s, t],
            )
            now.append(copy)
            low[s] = keep
        for s in range(streams):
            now[s].wait_recv()

            def add(i, _, s=s, src=src, offset=offset, last=t == steps - 1):
                place = low[s] + i
                total = (
                    src[s, place].astype(jnp.float32) + r_ref[s, offset + i].astype(jnp.float32)
                ).astype(jnp.bfloat16)
                if last:
                    put(s, place, total)
                else:
                    w_ref[s, place] = total
                return 0

            lax.fori_loop(0, half, add, 0)
        copies += now
        size = half
        offset += half
    return low, copies


def all_sum_kernel(axis, n, orders, gathers, x_ref, o_ref, w_ref, r_ref, send, recv):
    me = lax.axis_index(axis)
    steps = len(orders[0])
    streams = len(orders)
    greet(axis, me, list(range(steps)))

    def put(s, place, value):
        o_ref[s, place] = value

    low, copies = scatter_steps(axis, me, orders, n, x_ref, w_ref, r_ref, put, send, recv)
    size = 1
    for g in range(gathers):
        t = steps - 1 - g
        now = []
        for s in range(streams):
            part = o_ref.at[s, pl.ds(low[s], size)]
            now.append(
                remote(
                    axis, me, orders[s][t], part, part,
                    send.at[s, steps + g], recv.at[s, steps + g],
                )
            )
            low[s] = low[s] - ((me >> orders[s][t]) & 1) * size
        for copy in now:
            copy.wait_recv()
        copies += now
        size *= 2
    for copy in copies:
        copy.wait_send()


def all_sum(x, axis, n, orders, cid, gathers=None):
    rows, width = x.shape
    m = bits_of(n)
    gathers = m if gathers is None else gathers
    streams = len(orders)
    shape = (streams, n, rows // (streams * n), width)
    out = pl.pallas_call(
        functools.partial(all_sum_kernel, axis, n, orders, gathers),
        out_shape=jax.ShapeDtypeStruct(shape, jnp.bfloat16),
        in_specs=[pl.BlockSpec(memory_space=pltpu.VMEM)],
        out_specs=pl.BlockSpec(memory_space=pltpu.VMEM),
        scratch_shapes=[
            pltpu.VMEM(shape, jnp.bfloat16),
            pltpu.VMEM(shape, jnp.bfloat16),
            pltpu.SemaphoreType.DMA((streams, 2 * m)),
            pltpu.SemaphoreType.DMA((streams, 2 * m)),
        ],
        compiler_params=pltpu.CompilerParams(collective_id=cid, has_side_effects=True),
    )(x.reshape(shape))
    return out.reshape(rows, width)


def both_sum_kernel(axis, n, x_ref, o_ref, w_ref, r_ref, send, recv):
    me = lax.axis_index(axis)
    m = bits_of(n)
    slot = me >> (m - 1)
    greet(axis, me, list(range(m)))

    def put(s, place, value):
        o_ref[slot, place] = value

    order = list(range(m - 1))
    low, copies = scatter_steps(
        axis, me, [order], n // 2, x_ref, w_ref, r_ref, put, send, recv
    )
    place = low[0]
    part = o_ref.at[slot, pl.ds(place, 1)]
    cross = remote(axis, me, m - 1, part, part, send.at[0, m - 1], recv.at[0, m - 1])
    cross.wait_recv()
    copies.append(cross)
    size = 1
    for g in range(m - 1):
        bit = order[m - 2 - g]
        part = o_ref.at[:, pl.ds(place, size)]
        copy = remote(axis, me, bit, part, part, send.at[0, m + g], recv.at[0, m + g])
        place = place - ((me >> bit) & 1) * size
        copy.wait_recv()
        copies.append(copy)
        size *= 2
    for copy in copies:
        copy.wait_send()


def both_sum(x, axis, n, cid):
    rows, width = x.shape
    m = bits_of(n)
    half = n // 2
    chunk = rows // half
    out = pl.pallas_call(
        functools.partial(both_sum_kernel, axis, n),
        out_shape=jax.ShapeDtypeStruct((2, half, chunk, width), jnp.bfloat16),
        in_specs=[pl.BlockSpec(memory_space=pltpu.VMEM)],
        out_specs=pl.BlockSpec(memory_space=pltpu.VMEM),
        scratch_shapes=[
            pltpu.VMEM((1, half, chunk, width), jnp.bfloat16),
            pltpu.VMEM((1, half, chunk, width), jnp.bfloat16),
            pltpu.SemaphoreType.DMA((1, 2 * m)),
            pltpu.SemaphoreType.DMA((1, 2 * m)),
        ],
        compiler_params=pltpu.CompilerParams(collective_id=cid, has_side_effects=True),
    )(x.reshape(1, half, chunk, width))
    return out.reshape(2, rows, width)


def place_kernel(idx_ref, update_ref, given_ref, o_ref):
    def body(j, _):
        value = given_ref[j]
        for k in range(2):
            i = idx_ref[k, j]
            block = update_ref[jnp.maximum(i, 0)].astype(jnp.float32)
            value = value - jnp.where(i >= 0, block, 0.0)
        o_ref[j] = value.astype(jnp.bfloat16)
        return 0

    lax.fori_loop(0, o_ref.shape[0], body, 0)


def pick_kernel(idx_ref, rows_ref, o_ref):
    def body(j, _):
        i = idx_ref[j]
        block = rows_ref[jnp.maximum(i, 0)].astype(jnp.float32)
        o_ref[j] = jnp.where(i >= 0, block, 0.0).astype(jnp.bfloat16)
        return 0

    lax.fori_loop(0, o_ref.shape[0], body, 0)


def local(row_devices, col_devices, child_inverse, root_upper, coupling, child_rhs, root_rhs, child_map):
    row_place = lax.axis_index("row")
    col_place = lax.axis_index("col")
    child_slot = row_place // (row_devices // 2)
    root_rows = root_upper.shape[0]
    coupled = coupling.shape[0]
    rhs_width = child_rhs.shape[2]
    vmem = pl.BlockSpec(memory_space=pltpu.VMEM)
    smem = pl.BlockSpec(memory_space=pltpu.SMEM)
    row_bits = list(range(bits_of(row_devices)))
    col_bits = list(range(bits_of(col_devices)))
    col_orders = [col_bits, col_bits[:1] + col_bits[:0:-1]]
    row_orders = [row_bits, row_bits[::-1]]
    pick_order = [row_bits[-1:] + row_bits[:-1]]
    contract_first = (((0,), (0,)), ((), ()))

    per_col = coupled // BLK
    root_blocks = root_rows // BLK
    local_map = lax.dynamic_slice_in_dim(child_map, col_place * per_col, per_col, 1)
    target = local_map - row_place * root_blocks
    block_hits = target[:, :, None] == jnp.arange(root_blocks, dtype=jnp.int32)[None, None, :]
    slots = jnp.arange(2 * per_col, dtype=jnp.int32).reshape(2, per_col, 1)
    place_idx = jnp.max(jnp.where(block_hits, slots, -1), axis=1)
    pick_idx = jnp.where((target >= 0) & (target < root_blocks), target, -1).reshape(-1)
    rhs_rows = root_rhs.shape[0]
    given_rows = lax.dynamic_update_slice(
        jnp.zeros((root_rows, rhs_width), jnp.float32),
        root_rhs,
        (col_place * rhs_rows, jnp.int32(0)),
    )

    own_rhs = lax.dynamic_index_in_dim(child_rhs, child_slot, 1, keepdims=False).astype(
        jnp.bfloat16
    )
    child_low = all_sum(
        jnp.dot(child_inverse, own_rhs, preferred_element_type=jnp.float32).astype(jnp.bfloat16),
        "col", col_devices, col_orders, 0,
    )
    update = jnp.dot(coupling, child_low, preferred_element_type=jnp.float32)
    update_both = both_sum(update.astype(jnp.bfloat16), "row", row_devices, 1)
    root_term = pl.pallas_call(
        place_kernel,
        out_shape=jax.ShapeDtypeStruct((root_blocks, BLK, rhs_width), jnp.bfloat16),
        in_specs=[smem, vmem, vmem],
        out_specs=vmem,
    )(
        place_idx,
        update_both.reshape(2 * per_col, BLK, rhs_width),
        given_rows.reshape(root_blocks, BLK, rhs_width),
    )
    root_low = all_sum(
        root_term.reshape(root_rows, rhs_width), "col", col_devices, col_orders, 2
    )
    solved_low = all_sum(
        lax.dot_general(
            root_upper, root_low, contract_first, preferred_element_type=jnp.float32
        ).astype(jnp.bfloat16),
        "row", row_devices, row_orders, 3,
    )
    rows_low = all_sum(
        jnp.dot(root_upper, solved_low, preferred_element_type=jnp.float32).astype(jnp.bfloat16),
        "col", col_devices, col_orders, 4,
    )
    root_solution = lax.dynamic_slice_in_dim(rows_low, col_place * rhs_rows, rhs_rows, 0).astype(
        jnp.float32
    )
    picked = pl.pallas_call(
        pick_kernel,
        out_shape=jax.ShapeDtypeStruct((2 * per_col, BLK, rhs_width), jnp.bfloat16),
        in_specs=[smem, vmem],
        out_specs=vmem,
    )(pick_idx, rows_low.reshape(root_blocks, BLK, rhs_width))
    picked_half = all_sum(
        picked.reshape(2 * coupled, rhs_width), "row", row_devices, pick_order, 5,
        gathers=len(row_bits) - 1,
    )
    own_pick = lax.dynamic_slice_in_dim(picked_half, child_slot * coupled, coupled, 0)
    back_term = all_sum(
        lax.dot_general(
            coupling, own_pick, contract_first, preferred_element_type=jnp.float32
        ).astype(jnp.bfloat16),
        "col", col_devices, col_orders, 6,
    )
    adjusted = (child_low.astype(jnp.float32) - back_term.astype(jnp.float32)).astype(
        jnp.bfloat16
    )
    final_rows = lax.dot_general(
        child_inverse, adjusted, contract_first, preferred_element_type=jnp.float32
    )
    final_both = both_sum(final_rows.astype(jnp.bfloat16), "row", row_devices, 7)
    child_solution = jnp.transpose(final_both, (1, 0, 2)).astype(jnp.float32)
    return (root_solution, child_solution)


def solution(mesh):
    return jax.shard_map(
        functools.partial(local, mesh.shape["row"], mesh.shape["col"]),
        mesh=mesh,
        in_specs=(
            P("row", "col"),
            P("row", "col"),
            P("col", "row"),
            P("col", None, None),
            P(("row", "col"), None),
            P(),
        ),
        out_specs=(P(("row", "col"), None), P("col", None, None)),
        check_vma=False,
    )
```

```python
import functools

import jax
import jax.numpy as jnp
from jax import lax
from jax.experimental import pallas as pl
from jax.experimental.pallas import tpu as pltpu
from jax.sharding import PartitionSpec as P

BLK = 128
MESH = pl.DeviceIdType.MESH


def bits_of(n):
    m = n.bit_length() - 1
    assert 1 << m == n
    return m


def greet(axis, me, bits):
    barrier = pltpu.get_barrier_semaphore()
    for b in bits:
        pl.semaphore_signal(
            barrier, inc=1, device_id={axis: me ^ (1 << b)}, device_id_type=MESH
        )
    pl.semaphore_wait(barrier, len(bits))


def remote(axis, me, bit, src, dst, send, recv):
    copy = pltpu.make_async_remote_copy(
        src_ref=src,
        dst_ref=dst,
        send_sem=send,
        recv_sem=recv,
        device_id={axis: me ^ (1 << bit)},
        device_id_type=MESH,
    )
    copy.start()
    return copy


def run_streams(streams, steps, begin, finish):
    copies = [[begin(s, 0)] for s in range(streams)]
    for t in range(steps):
        for s in range(streams):
            copies[s][t].wait_recv()
            finish(s, t)
            if t + 1 < steps:
                copies[s].append(begin(s, t + 1))
    for own in copies:
        for copy in own:
            copy.wait_send()


def spans(me, order, n):
    low = jnp.int32(0)
    size = n
    offset = 0
    out = []
    for b in order:
        half = size // 2
        mine = (me >> b) & 1
        keep, away = low + mine * half, low + (1 - mine) * half
        out.append((keep, away, half, offset))
        low, size, offset = keep, half, offset + half
    return out


def add_landed(s, span, src, r_ref, put):
    keep, _, half, offset = span

    def add(i, _):
        total = src[s, keep + i].astype(jnp.float32) + r_ref[s, offset + i].astype(jnp.float32)
        put(keep + i, total.astype(jnp.bfloat16))
        return 0

    lax.fori_loop(0, half, add, 0)


def all_sum_kernel(axis, n, orders, gathers, x_ref, o_ref, w_ref, r_ref, send, recv):
    me = lax.axis_index(axis)
    steps = len(orders[0])
    plans = [spans(me, order, n) for order in orders]
    greet(axis, me, list(range(steps)))

    def begin(s, t):
        if t < steps:
            _, away, half, offset = plans[s][t]
            src = (x_ref if t == 0 else w_ref).at[s, pl.ds(away, half)]
            dst = r_ref.at[s, pl.ds(offset, half)]
            bit = orders[s][t]
        else:
            back = 2 * steps - 1 - t
            src = dst = o_ref.at[s, pl.ds(plans[s][back][0], plans[s][back][2])]
            bit = orders[s][back]
        return remote(axis, me, bit, src, dst, send.at[s, t], recv.at[s, t])

    def finish(s, t):
        if t < steps:

            def put(place, value):
                if t == steps - 1:
                    o_ref[s, place] = value
                else:
                    w_ref[s, place] = value

            add_landed(s, plans[s][t], x_ref if t == 0 else w_ref, r_ref, put)

    run_streams(len(orders), steps + gathers, begin, finish)


def all_sum(x, axis, n, orders, cid, gathers=None):
    rows, width = x.shape
    m = bits_of(n)
    gathers = m if gathers is None else gathers
    streams = len(orders)
    shape = (streams, n, rows // (streams * n), width)
    out = pl.pallas_call(
        functools.partial(all_sum_kernel, axis, n, orders, gathers),
        out_shape=jax.ShapeDtypeStruct(shape, jnp.bfloat16),
        in_specs=[pl.BlockSpec(memory_space=pltpu.VMEM)],
        out_specs=pl.BlockSpec(memory_space=pltpu.VMEM),
        scratch_shapes=[
            pltpu.VMEM(shape, jnp.bfloat16),
            pltpu.VMEM(shape, jnp.bfloat16),
            pltpu.SemaphoreType.DMA((streams, 2 * m)),
            pltpu.SemaphoreType.DMA((streams, 2 * m)),
        ],
        compiler_params=pltpu.CompilerParams(collective_id=cid, has_side_effects=True),
    )(x.reshape(shape))
    return out.reshape(rows, width)


def both_sum_kernel(axis, n, streams, x_ref, o_ref, w_ref, r_ref, send, recv):
    me = lax.axis_index(axis)
    m = bits_of(n)
    slot = me >> (m - 1)
    plan = spans(me, list(range(m - 1)), n // 2)
    greet(axis, me, list(range(m)))

    def begin(s, t):
        if t < m - 1:
            _, away, half, offset = plan[t]
            src = (x_ref if t == 0 else w_ref).at[s, pl.ds(away, half)]
            dst = r_ref.at[s, pl.ds(offset, half)]
            bit = t
        elif t == m - 1:
            src = dst = o_ref.at[slot, s, pl.ds(plan[-1][0], 1)]
            bit = m - 1
        else:
            bit = 2 * (m - 1) - t
            src = dst = o_ref.at[:, s, pl.ds(plan[bit][0], plan[bit][2])]
        return remote(axis, me, bit, src, dst, send.at[s, t], recv.at[s, t])

    def finish(s, t):
        if t < m - 1:

            def put(place, value):
                if t == m - 2:
                    o_ref[slot, s, place] = value
                else:
                    w_ref[s, place] = value

            add_landed(s, plan[t], x_ref if t == 0 else w_ref, r_ref, put)

    run_streams(streams, 2 * m - 1, begin, finish)


def both_sum(x, axis, n, streams, cid):
    rows, width = x.shape
    m = bits_of(n)
    half = n // 2
    shape = (streams, half, rows // (streams * half), width)
    out = pl.pallas_call(
        functools.partial(both_sum_kernel, axis, n, streams),
        out_shape=jax.ShapeDtypeStruct((2,) + shape, jnp.bfloat16),
        in_specs=[pl.BlockSpec(memory_space=pltpu.VMEM)],
        out_specs=pl.BlockSpec(memory_space=pltpu.VMEM),
        scratch_shapes=[
            pltpu.VMEM(shape, jnp.bfloat16),
            pltpu.VMEM(shape, jnp.bfloat16),
            pltpu.SemaphoreType.DMA((streams, 2 * m)),
            pltpu.SemaphoreType.DMA((streams, 2 * m)),
        ],
        compiler_params=pltpu.CompilerParams(collective_id=cid, has_side_effects=True),
    )(x.reshape(shape))
    return out.reshape(2, rows, width)


def place_kernel(idx_ref, update_ref, given_ref, o_ref):
    def body(j, _):
        value = given_ref[j]
        for k in range(2):
            i = idx_ref[k, j]
            block = update_ref[jnp.maximum(i, 0)].astype(jnp.float32)
            value = value - jnp.where(i >= 0, block, 0.0)
        o_ref[j] = value.astype(jnp.bfloat16)
        return 0

    lax.fori_loop(0, o_ref.shape[0], body, 0)


def pick_kernel(idx_ref, rows_ref, o_ref):
    def body(j, _):
        i = idx_ref[j]
        block = rows_ref[jnp.maximum(i, 0)].astype(jnp.float32)
        o_ref[j] = jnp.where(i >= 0, block, 0.0).astype(jnp.bfloat16)
        return 0

    lax.fori_loop(0, o_ref.shape[0], body, 0)


def local(row_devices, col_devices, child_inverse, root_upper, coupling, child_rhs, root_rhs, child_map):
    row_place = lax.axis_index("row")
    col_place = lax.axis_index("col")
    child_slot = row_place // (row_devices // 2)
    root_rows = root_upper.shape[0]
    coupled = coupling.shape[0]
    rhs_width = child_rhs.shape[2]
    vmem = pl.BlockSpec(memory_space=pltpu.VMEM)
    smem = pl.BlockSpec(memory_space=pltpu.SMEM)
    row_bits = list(range(bits_of(row_devices)))
    col_bits = list(range(bits_of(col_devices)))
    col_orders = [col_bits, col_bits[:1] + col_bits[:0:-1]] * 2
    row_orders = [row_bits, row_bits[::-1]] * 2
    pick_order = [row_bits[-1:] + row_bits[:-1]]
    contract_first = (((0,), (0,)), ((), ()))

    per_col = coupled // BLK
    root_blocks = root_rows // BLK
    local_map = lax.dynamic_slice_in_dim(child_map, col_place * per_col, per_col, 1)
    target = local_map - row_place * root_blocks
    block_hits = target[:, :, None] == jnp.arange(root_blocks, dtype=jnp.int32)[None, None, :]
    slots = jnp.arange(2 * per_col, dtype=jnp.int32).reshape(2, per_col, 1)
    place_idx = jnp.max(jnp.where(block_hits, slots, -1), axis=1)
    pick_idx = jnp.where((target >= 0) & (target < root_blocks), target, -1).reshape(-1)
    rhs_rows = root_rhs.shape[0]
    given_rows = lax.dynamic_update_slice(
        jnp.zeros((root_rows, rhs_width), jnp.float32),
        root_rhs,
        (col_place * rhs_rows, jnp.int32(0)),
    )

    own_rhs = lax.dynamic_index_in_dim(child_rhs, child_slot, 1, keepdims=False).astype(
        jnp.bfloat16
    )
    child_low = all_sum(
        jnp.dot(child_inverse, own_rhs, preferred_element_type=jnp.float32).astype(jnp.bfloat16),
        "col", col_devices, col_orders, 0,
    )
    update = jnp.dot(coupling, child_low, preferred_element_type=jnp.float32)
    update_both = both_sum(update.astype(jnp.bfloat16), "row", row_devices, 2, 1)
    root_term = pl.pallas_call(
        place_kernel,
        out_shape=jax.ShapeDtypeStruct((root_blocks, BLK, rhs_width), jnp.bfloat16),
        in_specs=[smem, vmem, vmem],
        out_specs=vmem,
    )(
        place_idx,
        update_both.reshape(2 * per_col, BLK, rhs_width),
        given_rows.reshape(root_blocks, BLK, rhs_width),
    )
    root_low = all_sum(
        root_term.reshape(root_rows, rhs_width), "col", col_devices, col_orders, 2
    )
    solved_low = all_sum(
        lax.dot_general(
            root_upper, root_low, contract_first, preferred_element_type=jnp.float32
        ).astype(jnp.bfloat16),
        "row", row_devices, row_orders, 3,
    )
    rows_low = all_sum(
        jnp.dot(root_upper, solved_low, preferred_element_type=jnp.float32).astype(jnp.bfloat16),
        "col", col_devices, col_orders, 4,
    )
    root_solution = lax.dynamic_slice_in_dim(rows_low, col_place * rhs_rows, rhs_rows, 0).astype(
        jnp.float32
    )
    picked = pl.pallas_call(
        pick_kernel,
        out_shape=jax.ShapeDtypeStruct((2 * per_col, BLK, rhs_width), jnp.bfloat16),
        in_specs=[smem, vmem],
        out_specs=vmem,
    )(pick_idx, rows_low.reshape(root_blocks, BLK, rhs_width))
    picked_half = all_sum(
        picked.reshape(2 * coupled, rhs_width), "row", row_devices, pick_order, 5,
        gathers=len(row_bits) - 1,
    )
    own_pick = lax.dynamic_slice_in_dim(picked_half, child_slot * coupled, coupled, 0)
    back_term = all_sum(
        lax.dot_general(
            coupling, own_pick, contract_first, preferred_element_type=jnp.float32
        ).astype(jnp.bfloat16),
        "col", col_devices, col_orders, 6,
    )
    adjusted = (child_low.astype(jnp.float32) - back_term.astype(jnp.float32)).astype(
        jnp.bfloat16
    )
    final_rows = lax.dot_general(
        child_inverse, adjusted, contract_first, preferred_element_type=jnp.float32
    )
    final_both = both_sum(final_rows.astype(jnp.bfloat16), "row", row_devices, 4, 7)
    child_solution = jnp.transpose(final_both, (1, 0, 2)).astype(jnp.float32)
    return (root_solution, child_solution)


def solution(mesh):
    return jax.shard_map(
        functools.partial(local, mesh.shape["row"], mesh.shape["col"]),
        mesh=mesh,
        in_specs=(
            P("row", "col"),
            P("row", "col"),
            P("col", "row"),
            P("col", None, None),
            P(("row", "col"), None),
            P(),
        ),
        out_specs=(P(("row", "col"), None), P("col", None, None)),
        check_vma=False,
    )
```

```python
import functools

import jax
import jax.numpy as jnp
from jax import lax
from jax.experimental import pallas as pl
from jax.experimental.pallas import tpu as pltpu
from jax.sharding import PartitionSpec as P

BLK = 128
MESH = pl.DeviceIdType.MESH


def bits_of(n):
    m = n.bit_length() - 1
    assert 1 << m == n
    return m


def greet(axis, me, bits):
    barrier = pltpu.get_barrier_semaphore()
    for b in bits:
        pl.semaphore_signal(
            barrier, inc=1, device_id={axis: me ^ (1 << b)}, device_id_type=MESH
        )
    pl.semaphore_wait(barrier, len(bits))


def remote(axis, me, bit, src, dst, send, recv):
    copy = pltpu.make_async_remote_copy(
        src_ref=src,
        dst_ref=dst,
        send_sem=send,
        recv_sem=recv,
        device_id={axis: me ^ (1 << bit)},
        device_id_type=MESH,
    )
    copy.start()
    return copy


def run_streams(streams, steps, begin, finish):
    copies = [[begin(s, 0)] for s in range(streams)]
    for t in range(steps):
        for s in range(streams):
            copies[s][t].wait_recv()
            finish(s, t)
            if t + 1 < steps:
                copies[s].append(begin(s, t + 1))
    for own in copies:
        for copy in own:
            copy.wait_send()


def spans(me, order, n):
    low = jnp.int32(0)
    size = n
    offset = 0
    out = []
    for b in order:
        half = size // 2
        mine = (me >> b) & 1
        keep, away = low + mine * half, low + (1 - mine) * half
        out.append((keep, away, half, offset))
        low, size, offset = keep, half, offset + half
    return out


def add_landed(s, span, src, r_ref, put):
    keep, _, half, offset = span

    def add(i, _):
        total = src[s, keep + i].astype(jnp.float32) + r_ref[s, offset + i].astype(jnp.float32)
        put(keep + i, total.astype(jnp.bfloat16))
        return 0

    lax.fori_loop(0, half, add, 0)


def all_sum_kernel(axis, n, orders, gathers, x_ref, o_ref, w_ref, r_ref, send, recv):
    me = lax.axis_index(axis)
    steps = len(orders[0])
    plans = [spans(me, order, n) for order in orders]
    greet(axis, me, list(range(steps)))

    def begin(s, t):
        if t < steps:
            _, away, half, offset = plans[s][t]
            src = (x_ref if t == 0 else w_ref).at[s, pl.ds(away, half)]
            dst = r_ref.at[s, pl.ds(offset, half)]
            bit = orders[s][t]
        else:
            back = 2 * steps - 1 - t
            src = dst = o_ref.at[s, pl.ds(plans[s][back][0], plans[s][back][2])]
            bit = orders[s][back]
        return remote(axis, me, bit, src, dst, send.at[s, t], recv.at[s, t])

    def finish(s, t):
        if t < steps:

            def put(place, value):
                if t == steps - 1:
                    o_ref[s, place] = value
                else:
                    w_ref[s, place] = value

            add_landed(s, plans[s][t], x_ref if t == 0 else w_ref, r_ref, put)

    run_streams(len(orders), steps + gathers, begin, finish)


def all_sum(x, axis, n, orders, cid, gathers=None):
    rows, width = x.shape
    m = bits_of(n)
    gathers = m if gathers is None else gathers
    streams = len(orders)
    shape = (streams, n, rows // (streams * n), width)
    out = pl.pallas_call(
        functools.partial(all_sum_kernel, axis, n, orders, gathers),
        out_shape=jax.ShapeDtypeStruct(shape, jnp.bfloat16),
        in_specs=[pl.BlockSpec(memory_space=pltpu.VMEM)],
        out_specs=pl.BlockSpec(memory_space=pltpu.VMEM),
        scratch_shapes=[
            pltpu.VMEM(shape, jnp.bfloat16),
            pltpu.VMEM(shape, jnp.bfloat16),
            pltpu.SemaphoreType.DMA((streams, 2 * m)),
            pltpu.SemaphoreType.DMA((streams, 2 * m)),
        ],
        compiler_params=pltpu.CompilerParams(collective_id=cid, has_side_effects=True),
    )(x.reshape(shape))
    return out.reshape(rows, width)


def both_sum_kernel(axis, n, streams, x_ref, o_ref, w_ref, r_ref, send, recv):
    me = lax.axis_index(axis)
    m = bits_of(n)
    slot = me >> (m - 1)
    plan = spans(me, list(range(m - 1)), n // 2)
    greet(axis, me, list(range(m)))

    def begin(s, t):
        if t < m - 1:
            _, away, half, offset = plan[t]
            src = (x_ref if t == 0 else w_ref).at[s, pl.ds(away, half)]
            dst = r_ref.at[s, pl.ds(offset, half)]
            bit = t
        elif t == m - 1:
            src = dst = o_ref.at[slot, s, pl.ds(plan[-1][0], 1)]
            bit = m - 1
        else:
            bit = 2 * (m - 1) - t
            src = dst = o_ref.at[:, s, pl.ds(plan[bit][0], plan[bit][2])]
        return remote(axis, me, bit, src, dst, send.at[s, t], recv.at[s, t])

    def finish(s, t):
        if t < m - 1:

            def put(place, value):
                if t == m - 2:
                    o_ref[slot, s, place] = value
                else:
                    w_ref[s, place] = value

            add_landed(s, plan[t], x_ref if t == 0 else w_ref, r_ref, put)

    run_streams(streams, 2 * m - 1, begin, finish)


def both_sum(x, axis, n, streams, cid):
    rows, width = x.shape
    m = bits_of(n)
    half = n // 2
    shape = (streams, half, rows // (streams * half), width)
    out = pl.pallas_call(
        functools.partial(both_sum_kernel, axis, n, streams),
        out_shape=jax.ShapeDtypeStruct((2,) + shape, jnp.bfloat16),
        in_specs=[pl.BlockSpec(memory_space=pltpu.VMEM)],
        out_specs=pl.BlockSpec(memory_space=pltpu.VMEM),
        scratch_shapes=[
            pltpu.VMEM(shape, jnp.bfloat16),
            pltpu.VMEM(shape, jnp.bfloat16),
            pltpu.SemaphoreType.DMA((streams, 2 * m)),
            pltpu.SemaphoreType.DMA((streams, 2 * m)),
        ],
        compiler_params=pltpu.CompilerParams(collective_id=cid, has_side_effects=True),
    )(x.reshape(shape))
    return out.reshape(2, rows, width)


def place_kernel(idx_ref, update_ref, given_ref, o_ref):
    def body(j, _):
        value = given_ref[j]
        for k in range(2):
            i = idx_ref[k, j]
            block = update_ref[jnp.maximum(i, 0)].astype(jnp.float32)
            value = value - jnp.where(i >= 0, block, 0.0)
        o_ref[j] = value.astype(jnp.bfloat16)
        return 0

    lax.fori_loop(0, o_ref.shape[0], body, 0)


def pick_kernel(idx_ref, rows_ref, o_ref):
    def body(j, _):
        i = idx_ref[j]
        block = rows_ref[jnp.maximum(i, 0)].astype(jnp.float32)
        o_ref[j] = jnp.where(i >= 0, block, 0.0).astype(jnp.bfloat16)
        return 0

    lax.fori_loop(0, o_ref.shape[0], body, 0)


def weave_kernel(x_ref, o_ref):
    step = 64

    def body(i, _):
        rows = pl.ds(pl.multiple_of(i * step, step), step)
        for k in range(2):
            o_ref[rows, k, :] = x_ref[k, rows, :].astype(jnp.float32)
        return 0

    lax.fori_loop(0, o_ref.shape[0] // step, body, 0)


def local(row_devices, col_devices, child_inverse, root_upper, coupling, child_rhs, root_rhs, child_map):
    row_place = lax.axis_index("row")
    col_place = lax.axis_index("col")
    child_slot = row_place // (row_devices // 2)
    root_rows = root_upper.shape[0]
    coupled = coupling.shape[0]
    rhs_width = child_rhs.shape[2]
    vmem = pl.BlockSpec(memory_space=pltpu.VMEM)
    smem = pl.BlockSpec(memory_space=pltpu.SMEM)
    row_bits = list(range(bits_of(row_devices)))
    col_bits = list(range(bits_of(col_devices)))
    col_orders = [col_bits, col_bits[:1] + col_bits[:0:-1]] * 2
    row_orders = [row_bits, row_bits[::-1]] * 2
    pick_order = [row_bits[-1:] + row_bits[:-1]]
    contract_first = (((0,), (0,)), ((), ()))

    per_col = coupled // BLK
    root_blocks = root_rows // BLK
    local_map = lax.dynamic_slice_in_dim(child_map, col_place * per_col, per_col, 1)
    target = local_map - row_place * root_blocks
    block_hits = target[:, :, None] == jnp.arange(root_blocks, dtype=jnp.int32)[None, None, :]
    slots = jnp.arange(2 * per_col, dtype=jnp.int32).reshape(2, per_col, 1)
    place_idx = jnp.max(jnp.where(block_hits, slots, -1), axis=1)
    pick_idx = jnp.where((target >= 0) & (target < root_blocks), target, -1).reshape(-1)
    rhs_rows = root_rhs.shape[0]
    given_rows = lax.dynamic_update_slice(
        jnp.zeros((root_rows, rhs_width), jnp.float32),
        root_rhs,
        (col_place * rhs_rows, jnp.int32(0)),
    )

    own_rhs = lax.dynamic_index_in_dim(child_rhs, child_slot, 1, keepdims=False).astype(
        jnp.bfloat16
    )
    child_low = all_sum(
        jnp.dot(child_inverse, own_rhs, preferred_element_type=jnp.float32).astype(jnp.bfloat16),
        "col", col_devices, col_orders, 0,
    )
    update = jnp.dot(coupling, child_low, preferred_element_type=jnp.float32)
    update_both = both_sum(update.astype(jnp.bfloat16), "row", row_devices, 2, 1)
    root_term = pl.pallas_call(
        place_kernel,
        out_shape=jax.ShapeDtypeStruct((root_blocks, BLK, rhs_width), jnp.bfloat16),
        in_specs=[smem, vmem, vmem],
        out_specs=vmem,
    )(
        place_idx,
        update_both.reshape(2 * per_col, BLK, rhs_width),
        given_rows.reshape(root_blocks, BLK, rhs_width),
    )
    root_low = all_sum(
        root_term.reshape(root_rows, rhs_width), "col", col_devices, col_orders, 2
    )
    solved_low = all_sum(
        lax.dot_general(
            root_upper, root_low, contract_first, preferred_element_type=jnp.float32
        ).astype(jnp.bfloat16),
        "row", row_devices, row_orders, 3,
    )
    rows_low = all_sum(
        jnp.dot(root_upper, solved_low, preferred_element_type=jnp.float32).astype(jnp.bfloat16),
        "col", col_devices, col_orders, 4,
    )
    root_solution = lax.dynamic_slice_in_dim(rows_low, col_place * rhs_rows, rhs_rows, 0).astype(
        jnp.float32
    )
    picked = pl.pallas_call(
        pick_kernel,
        out_shape=jax.ShapeDtypeStruct((2 * per_col, BLK, rhs_width), jnp.bfloat16),
        in_specs=[smem, vmem],
        out_specs=vmem,
    )(pick_idx, rows_low.reshape(root_blocks, BLK, rhs_width))
    picked_half = all_sum(
        picked.reshape(2 * coupled, rhs_width), "row", row_devices, pick_order, 5,
        gathers=len(row_bits) - 1,
    )
    own_pick = lax.dynamic_slice_in_dim(picked_half, child_slot * coupled, coupled, 0)
    back_term = all_sum(
        lax.dot_general(
            coupling, own_pick, contract_first, preferred_element_type=jnp.float32
        ).astype(jnp.bfloat16),
        "col", col_devices, col_orders, 6,
    )
    adjusted = (child_low.astype(jnp.float32) - back_term.astype(jnp.float32)).astype(
        jnp.bfloat16
    )
    final_rows = lax.dot_general(
        child_inverse, adjusted, contract_first, preferred_element_type=jnp.float32
    )
    final_both = both_sum(final_rows.astype(jnp.bfloat16), "row", row_devices, 4, 7)
    child_solution = pl.pallas_call(
        weave_kernel,
        out_shape=jax.ShapeDtypeStruct(child_rhs.shape, jnp.float32),
        in_specs=[vmem],
        out_specs=vmem,
    )(final_both)
    return (root_solution, child_solution)


def solution(mesh):
    return jax.shard_map(
        functools.partial(local, mesh.shape["row"], mesh.shape["col"]),
        mesh=mesh,
        in_specs=(
            P("row", "col"),
            P("row", "col"),
            P("col", "row"),
            P("col", None, None),
            P(("row", "col"), None),
            P(),
        ),
        out_specs=(P(("row", "col"), None), P("col", None, None)),
        check_vma=False,
    )
```
